32 devices in a mesh: grp: 2 (over y), site: 4 (over x, core), spin: 4 (over z).
Axes of the slice: x: 2, y: 2, z: 4, core: 2. Of those that a mesh axis runs over, the one named last changes fastest.
Arguments:
- walkers: bfloat16 [8, 512, 256, 256], P(('grp', 'spin'), 'site'), parts along dimension 0, may hold values from -90 to 90
- fields: bfloat16 [8, 1, 512, 256], P(('grp', 'spin'), None, 'site'), parts along dimension 0, may hold values from -3 to 3
- kinetic_x: bfloat16 [512, 512], replicated, may hold values from -0.5 to 1.5
- kinetic_y: bfloat16 [256, 256], replicated, may hold values from -0.5 to 1.5
Outputs:
- orthonormal: bfloat16 [8, 512, 256, 256], P(('grp', 'spin'), 'site'), parts along dimension 0
- triangle: float32 [8, 256, 256], P(('grp', 'spin')), parts along dimension 0
The draws below stay inside these ranges and needn't reach their ends.
There are 2 independent parts, one for each index of `grp`. The reference program is written for one: setup_inputs(seed, part) draws one part's arguments, and reference() takes and returns one part's arrays. A program takes and returns all parts, laid end to end along the dimension named above; an argument that names none is the same for every part. Nothing has to cross between parts.
All inputs are finite; a program needn't handle non-finite values.
Results may differ from the reference program's by a relative error of at most 0.0095.
Values may be sent and summed in bfloat16 or wider, within the bound.
A program may use at most 128 MiB of HBM per device.

```python
import math
import jax
import jax.numpy as jnp
from jax import lax

LX = 512
LY = 256
ORBS = 256
STEPS = 1
SLOTS = 4


def kinetic_matrix(key, count):
    noise = jnp.clip(jax.random.normal(key, (count, count), jnp.float32), -6.0, 6.0)
    return (jnp.eye(count, dtype=jnp.float32) + 0.3 * noise / math.sqrt(count)).astype(jnp.bfloat16)


def draw_kinetic_x(key, part):
    return kinetic_matrix(jax.random.fold_in(key, 11), LX)


def draw_kinetic_y(key, part):
    return kinetic_matrix(jax.random.fold_in(key, 23), LY)


def draw_walkers(key, part):
    base_key, rough_key, column_key = jax.random.split(jax.random.fold_in(key, 37), 3)
    shape = (SLOTS, LX, LY, ORBS)
    base = jnp.clip(jax.random.normal(base_key, shape, jnp.float32), -6.0, 6.0)
    rise = jnp.exp(math.log(3.0) * jnp.arange(LX, dtype=jnp.float32) / (LX - 1))
    rough = jnp.exp(jax.random.uniform(rough_key, (SLOTS, LX, LY, 1), jnp.float32, 0.0, math.log(3.3)))
    columns = jnp.exp(jax.random.uniform(column_key, (SLOTS, 1, 1, ORBS), jnp.float32, math.log(0.3), math.log(3.0)))
    values = 0.5 * base * rise[None, :, None, None] * rough * columns
    return values.astype(jnp.bfloat16)


def level_of(own_key, extent, pieces, least, high):
    gain, own = 1.0, jax.random.fold_in(own_key, 6)
    for dim, shards_of in pieces:
        steps = jnp.exp(jax.random.uniform(jax.random.fold_in(own, dim), (shards_of,), jnp.float32, least / len(pieces), high / len(pieces)))
        gain = gain * jnp.repeat(steps, extent[dim] // shards_of).reshape([-1 if axis == dim else 1 for axis in range(len(extent))])
    return gain


def normal_values(key, dims, deviation, most, pieces=(), kind=jnp.bfloat16):
    array = jax.random.normal(key, dims, jnp.float32) * deviation
    if len(pieces) > 0:
        array = level_of(key, dims, pieces, -0.22, 0.18) * array
    return jnp.clip(array, min=-most, max=most).astype(kind)


def setup_inputs(seed: int = 0, part: int = 0) -> dict:
    keys = jax.random.split(jax.random.key(seed), 5)
    part_keys = jax.random.split(jax.random.fold_in(keys[4], part), 5)
    walkers = draw_walkers(jax.random.fold_in(jax.random.fold_in(keys[4], part), 71), part)
    fields = normal_values(part_keys[1], (SLOTS, STEPS, LX, LY), 0.4, 3.0, ((0, 4), (2, 4)))
    kinetic_x = draw_kinetic_x(jax.random.fold_in(keys[4], 71), part)
    kinetic_y = draw_kinetic_y(jax.random.fold_in(keys[4], 71), part)
    return dict(walkers=walkers, fields=fields, kinetic_x=kinetic_x, kinetic_y=kinetic_y)


def one_slot(walker, field, kinetic_x, kinetic_y):
    current = walker
    for step in range(STEPS):
        after_y = jnp.einsum('yz,xzm->xym', kinetic_y.astype(jnp.float32), current.astype(jnp.float32)).astype(jnp.bfloat16)
        flat_y = after_y.reshape(LX, LY * ORBS)
        after_x = jnp.dot(kinetic_x.astype(jnp.float32), flat_y.astype(jnp.float32), preferred_element_type=jnp.float32).astype(jnp.bfloat16).reshape(LX, LY, ORBS)
        factor = jnp.exp(field[step].astype(jnp.float32))
        current = (factor[:, :, None] * after_x.astype(jnp.float32)).astype(jnp.bfloat16)
    flat = current.reshape(LX * LY, ORBS)
    gram = jnp.dot(flat.T.astype(jnp.float32), flat.astype(jnp.float32), preferred_element_type=jnp.float32) * (1.0 / (LX * LY))
    lower = jnp.linalg.cholesky(gram)
    identity = jnp.eye(ORBS, dtype=jnp.float32)
    inverse = jax.scipy.linalg.solve_triangular(lower, identity, lower=True).T
    inverse_half = inverse.astype(jnp.bfloat16)
    result = jnp.dot(flat.astype(jnp.float32), inverse_half.astype(jnp.float32), preferred_element_type=jnp.float32).astype(jnp.bfloat16)
    return (result.reshape(LX, LY, ORBS), lower)

def reference(walkers, fields, kinetic_x, kinetic_y):

    def apply_one(pair):
        return one_slot(pair[0], pair[1], kinetic_x, kinetic_y)
    orthonormal, triangle = lax.map(apply_one, (walkers, fields))
    return (orthonormal, triangle)
```

```python
import functools

import jax
import jax.numpy as jnp
from jax import lax
from jax.experimental import pallas as pl
from jax.experimental.pallas import tpu as pltpu
from jax.sharding import PartitionSpec as P

CORES = 2
LANES = 128
TILE = 16
CHUNKS = 4
VMEM = 48 * 1024 * 1024


def put(acc, row, value):
    for lane in range(acc.shape[0]):
        acc[lane, row : row + value.shape[0], :] = value[:, lane * LANES : (lane + 1) * LANES]


def take(acc, row, count, stride, out, place):
    for lane in range(acc.shape[0]):
        out[place, :, lane * LANES : (lane + 1) * LANES] = acc[
            lane, pl.ds(row, count, stride=stride), :
        ].astype(jnp.bfloat16)


def y_body(parts, rows, sites, k_ref, w_ref, *rest):
    outs, acc = rest[:parts], rest[parts]
    every = parts * rows
    for x in range(sites):
        put(acc, x * every, jnp.dot(k_ref[...], w_ref[x], preferred_element_type=jnp.float32))
    for part in range(parts):
        for y in range(rows):
            take(acc, part * rows + y, sites, every, outs[part], y)


def apply_y(walker, kinetic, parts):
    own, depth, orbitals = walker.shape
    every = kinetic.shape[0]
    rows = every // parts
    return pl.pallas_call(
        functools.partial(y_body, parts, rows, TILE),
        grid=(own // TILE,),
        in_specs=[
            pl.BlockSpec((every, depth), lambda i: (0, 0)),
            pl.BlockSpec((TILE, depth, orbitals), lambda i: (i, 0, 0)),
        ],
        out_specs=[pl.BlockSpec((rows, TILE, orbitals), lambda i: (0, i, 0))] * parts,
        out_shape=[jax.ShapeDtypeStruct((rows, own, orbitals), jnp.bfloat16)] * parts,
        scratch_shapes=[pltpu.VMEM((orbitals // LANES, TILE * every, LANES), jnp.float32)],
        compiler_params=pltpu.CompilerParams(vmem_limit_bytes=VMEM),
        cost_estimate=pl.CostEstimate(
            flops=2 * every * own * depth * orbitals,
            bytes_accessed=2 * own * orbitals * (depth + every),
            transcendentals=0,
        ),
        name="apply_y",
    )(kinetic, walker)


def x_body(count, lines, own, k_ref, f_ref, *refs):
    ins, outs, gram = refs[:count], refs[count : 2 * count], refs[2 * count]

    @pl.when(pl.program_id(0) == 0)
    def _():
        gram[...] = jnp.zeros_like(gram)

    total = None
    for y in range(lines):
        column = jnp.concatenate([r[y] for r in ins], axis=0)
        moved = jnp.dot(k_ref[...], column, preferred_element_type=jnp.float32)
        factor = f_ref[0, :, y : y + 1]
        out = (factor * moved.astype(jnp.bfloat16).astype(jnp.float32)).astype(jnp.bfloat16)
        for e in range(count):
            outs[e][y] = out[e * own : (e + 1) * own]
        part = lax.dot_general(out, out, (((0,), (0,)), ((), ())), preferred_element_type=jnp.float32)
        total = part if total is None else total + part
    gram[...] += total


def apply_x(columns, kinetic, factor, lines):
    count = len(columns)
    rows, own, orbitals = columns[0].shape
    every = count * own
    block = pl.BlockSpec((lines, own, orbitals), lambda i: (i, 0, 0))
    outs = pl.pallas_call(
        functools.partial(x_body, count, lines, own),
        grid=(rows // lines,),
        in_specs=[
            pl.BlockSpec((every, every), lambda i: (0, 0)),
            pl.BlockSpec((1, every, lines), lambda i: (i, 0, 0)),
        ]
        + [block] * count,
        out_specs=[block] * count + [pl.BlockSpec((orbitals, orbitals), lambda i: (0, 0))],
        out_shape=[jax.ShapeDtypeStruct((rows, own, orbitals), jnp.bfloat16)] * count
        + [jax.ShapeDtypeStruct((orbitals, orbitals), jnp.float32)],
        compiler_params=pltpu.CompilerParams(vmem_limit_bytes=VMEM),
        cost_estimate=pl.CostEstimate(
            flops=2 * rows * every * orbitals * (every + orbitals),
            bytes_accessed=4 * rows * every * orbitals,
            transcendentals=0,
        ),
        name="apply_x",
    )(kinetic, factor, *columns)
    return outs[:count], outs[count]


def out_body(lines, own, base_ref, p_ref, v_ref, *rest):
    out, acc = rest[-2], rest[-1]
    for y in range(lines):
        put(acc, y * own, jnp.dot(p_ref[y], v_ref[...], preferred_element_type=jnp.float32))
    for x in range(own):
        take(acc, x, lines, own, out, x)


def orthonormal_rows(part, inverse, base, result, shape):
    rows, own, orbitals = part.shape
    lines = TILE
    specs = [
        pl.BlockSpec((lines, own, orbitals), lambda i, b: (i, 0, 0)),
        pl.BlockSpec((orbitals, orbitals), lambda i, b: (0, 0)),
    ]
    operands = [part, inverse]
    aliases = {}
    if result is not None:
        specs.append(pl.BlockSpec(memory_space=pl.ANY))
        operands.append(result)
        aliases = {3: 0}
    return pl.pallas_call(
        functools.partial(out_body, lines, own),
        grid_spec=pltpu.PrefetchScalarGridSpec(
            num_scalar_prefetch=1,
            grid=(rows // lines,),
            in_specs=specs,
            out_specs=pl.BlockSpec((own, lines, orbitals), lambda i, b: (0, b[0] + i, 0)),
            scratch_shapes=[pltpu.VMEM((orbitals // LANES, lines * own, LANES), jnp.float32)],
        ),
        out_shape=jax.ShapeDtypeStruct(shape, jnp.bfloat16),
        input_output_aliases=aliases,
        compiler_params=pltpu.CompilerParams(vmem_limit_bytes=VMEM),
        cost_estimate=pl.CostEstimate(
            flops=2 * rows * own * orbitals * orbitals,
            bytes_accessed=4 * rows * own * orbitals,
            transcendentals=0,
        ),
        name="orthonormal_rows",
    )(base.reshape(1), *operands)


def factorize(gram):
    lower = jnp.linalg.cholesky(gram)
    identity = jnp.eye(gram.shape[-1], dtype=jnp.float32)
    inverse = jax.scipy.linalg.solve_triangular(lower, identity, lower=True).T
    return lower, inverse.astype(jnp.bfloat16)


def one_walker(count, walker, field, kinetic_x, kinetic_y):
    me = lax.axis_index("site")
    own, depth, orbitals = walker.shape
    share = depth // count
    chunks = max(1, min(CHUNKS, share // TILE))
    rows = share // chunks
    lines = min(8, rows)
    far = [d for d in range(count) if d >= CORES]
    near = [d for d in range(count) if d < CORES]

    def swap(value, d):
        return lax.ppermute(value, "site", [(s, s ^ d) for s in range(count)]) if d else value

    def rows_of(d, c):
        return lax.dynamic_slice_in_dim(kinetic_y, (me ^ d) * share + c * rows, rows, 0)

    fields = [
        swap(lax.dynamic_slice_in_dim(field, (me ^ d) * share, share, 1), d) for d in range(count)
    ]
    order = [
        lax.dynamic_slice_in_dim(kinetic_x, (me ^ d) * own, own, 0) for d in range(count)
    ]
    order = jnp.concatenate(order, axis=0)
    order = jnp.concatenate(
        [lax.dynamic_slice_in_dim(order, (me ^ d) * own, own, 1) for d in range(count)], axis=1
    )
    factor = jnp.exp(jnp.concatenate(fields, axis=0).astype(jnp.float32))
    factor = factor.reshape(count * own, share // lines, lines).swapaxes(0, 1)

    blocks = [[None] * count for _ in range(chunks)]
    for c in range(chunks):
        sent = apply_y(walker, jnp.concatenate([rows_of(d, c) for d in far], axis=0), len(far))
        for d, value in zip(far, sent):
            blocks[c][d] = swap(value, d)
    pairs = [(d, c) for c in range(chunks) for d in near]
    sent = apply_y(walker, jnp.concatenate([rows_of(d, c) for d, c in pairs], axis=0), len(pairs))
    for (d, c), value in zip(pairs, sent):
        blocks[c][d] = swap(value, d)

    scaled, gram = [], None
    per = rows // lines
    for c in range(chunks):
        outs, part = apply_x(blocks[c], order, factor[c * per : (c + 1) * per], lines)
        scaled.append(outs)
        gram = part if gram is None else gram + part
    gram = gram * (1.0 / (count * own * depth))
    step = 1
    while step < count:
        gram = gram + swap(gram, step)
        step *= 2

    home = [[swap(scaled[c][e], e) for e in range(count)] for c in range(chunks)]
    lower, inverse = factorize(gram)
    result = None
    for c in range(chunks):
        for e in near + far:
            base = ((me ^ e) * share + c * rows) // TILE
            result = orthonormal_rows(home[c][e], inverse, base, result, walker.shape)
    return result, lower


def per_device(count, walkers, fields, kinetic_x, kinetic_y):
    results, lowers = [], []
    for w in range(walkers.shape[0]):
        result, lower = one_walker(count, walkers[w], fields[w, 0], kinetic_x, kinetic_y)
        results.append(result[None])
        lowers.append(lower[None])
    return jnp.concatenate(results, axis=0), jnp.concatenate(lowers, axis=0)


def solution(mesh):
    placed = (
        P(("grp", "spin"), "site", None, None),
        P(("grp", "spin"), None, "site", None),
        P(),
        P(),
    )
    return jax.shard_map(
        functools.partial(per_device, mesh.shape["site"]),
        mesh=mesh,
        in_specs=placed,
        out_specs=(P(("grp", "spin"), "site", None, None), P(("grp", "spin"), None, None)),
        check_vma=False,
    )
```

```python
import functools

import jax
import jax.numpy as jnp
from jax import lax
from jax.experimental import pallas as pl
from jax.experimental.pallas import tpu as pltpu
from jax.sharding import PartitionSpec as P

CORES = 2
LANES = 128
TILE = 16
CHUNKS = 4
UNROLL = 8
LINES = 4
VMEM = 48 * 1024 * 1024


def put(acc, row, value):
    for lane in range(acc.shape[0]):
        acc[lane, row : row + value.shape[0], :] = value[:, lane * LANES : (lane + 1) * LANES]


def take(acc, row, count, stride, out, place):
    for lane in range(acc.shape[0]):
        out[place, :, lane * LANES : (lane + 1) * LANES] = acc[
            lane, pl.ds(row, count, stride=stride), :
        ].astype(jnp.bfloat16)


def y_body(parts, rows, sites, base_ref, *refs):
    kinetic, w_ref, outs, acc = refs[:parts], refs[parts], refs[-parts - 1 : -1], refs[-1]
    every = parts * rows
    left = jnp.concatenate([k[...] for k in kinetic], axis=0)

    for x in range(sites):
        put(acc, x * every, jnp.dot(left, w_ref[x], preferred_element_type=jnp.float32))

    for part in range(parts):

        @pl.loop(0, rows, step=UNROLL)
        def _(first, part=part):
            for y in range(UNROLL):
                take(acc, part * rows + first + y, sites, every, outs[part], first + y)


def apply_y(walker, kinetic, bases, rows, after):
    own, depth, orbitals = walker.shape
    parts = len(bases)
    every = rows * parts
    specs = [pl.BlockSpec((rows, depth), lambda i, b, p=p: (b[p], 0)) for p in range(parts)]
    specs.append(pl.BlockSpec((TILE, depth, orbitals), lambda i, b: (i, 0, 0)))
    operands = [kinetic] * parts + [walker]
    if after is not None:
        specs.append(pl.BlockSpec(memory_space=pl.ANY))
        operands.append(after)
    return pl.pallas_call(
        functools.partial(y_body, parts, rows, TILE),
        grid_spec=pltpu.PrefetchScalarGridSpec(
            num_scalar_prefetch=1,
            grid=(own // TILE,),
            in_specs=specs,
            out_specs=[pl.BlockSpec((rows, TILE, orbitals), lambda i, b: (0, i, 0))] * parts,
            scratch_shapes=[pltpu.VMEM((orbitals // LANES, TILE * every, LANES), jnp.float32)],
        ),
        out_shape=[jax.ShapeDtypeStruct((rows, own, orbitals), jnp.bfloat16)] * parts,
        compiler_params=pltpu.CompilerParams(vmem_limit_bytes=VMEM),
        cost_estimate=pl.CostEstimate(
            flops=2 * every * own * depth * orbitals,
            bytes_accessed=2 * own * orbitals * (depth + every),
            transcendentals=0,
        ),
        name="apply_y",
    )(jnp.stack(bases) // rows, *operands)


def x_body(count, lines, own, k_ref, f_ref, g_ref, *refs):
    ins, outs, gram = refs[:count], refs[count : 2 * count], refs[2 * count]

    @pl.when(pl.program_id(0) == 0)
    def _():
        gram[...] = g_ref[...]

    total = None
    for y in range(lines):
        column = jnp.concatenate([r[y] for r in ins], axis=0)
        moved = jnp.dot(k_ref[...], column, preferred_element_type=jnp.float32)
        factor = f_ref[0, :, y : y + 1]
        out = (factor * moved.astype(jnp.bfloat16).astype(jnp.float32)).astype(jnp.bfloat16)
        for e in range(count):
            outs[e][y] = out[e * own : (e + 1) * own]
        part = lax.dot_general(out, out, (((0,), (0,)), ((), ())), preferred_element_type=jnp.float32)
        total = part if total is None else total + part
    gram[...] += total


def apply_x(columns, kinetic, factor, gram, lines):
    count = len(columns)
    rows, own, orbitals = columns[0].shape
    every = count * own
    block = pl.BlockSpec((lines, own, orbitals), lambda i: (i, 0, 0))
    outs = pl.pallas_call(
        functools.partial(x_body, count, lines, own),
        grid=(rows // lines,),
        in_specs=[
            pl.BlockSpec((every, every), lambda i: (0, 0)),
            pl.BlockSpec((1, every, lines), lambda i: (i, 0, 0)),
            pl.BlockSpec((orbitals, orbitals), lambda i: (0, 0)),
        ]
        + [block] * count,
        out_specs=[block] * count + [pl.BlockSpec((orbitals, orbitals), lambda i: (0, 0))],
        out_shape=[jax.ShapeDtypeStruct((rows, own, orbitals), jnp.bfloat16)] * count
        + [jax.ShapeDtypeStruct((orbitals, orbitals), jnp.float32)],
        compiler_params=pltpu.CompilerParams(vmem_limit_bytes=VMEM),
        cost_estimate=pl.CostEstimate(
            flops=2 * rows * every * orbitals * (every + orbitals),
            bytes_accessed=4 * rows * every * orbitals,
            transcendentals=0,
        ),
        name="apply_x",
    )(kinetic, factor, gram, *columns)
    return outs[:count], outs[count]


def out_body(parts, steps, lines, sites, base_ref, *refs):
    ins, v_ref, out, held, acc = refs[:parts], refs[parts], refs[-3], refs[-2], refs[-1]
    for p in range(parts):

        @pl.when(pl.program_id(0) // steps == p)
        def _(p=p):
            held[...] = ins[p][...]

    @pl.loop(0, lines, step=4)
    def _(first):
        for y in range(4):
            row = pl.multiple_of((first + y) * sites, sites)
            value = jnp.dot(held[first + y], v_ref[...], preferred_element_type=jnp.float32)
            for lane in range(acc.shape[0]):
                acc[lane, pl.ds(row, sites), :] = value[:, lane * LANES : (lane + 1) * LANES]

    @pl.loop(0, sites, step=UNROLL)
    def _(first):
        for x in range(UNROLL):
            take(acc, first + x, lines, sites, out, first + x)


def orthonormal_rows(pieces, inverse, bases, result, shape):
    parts = len(pieces)
    rows, own, orbitals = pieces[0].shape
    lines, sites = TILE, min(own, 32)
    across = own // sites
    steps = (rows // lines) * across

    def piece_at(p):
        def at(i, b):
            j = jnp.clip(i - p * steps, 0, steps - 1)
            return (j // across, j % across, 0)

        return at

    def out_at(i, b):
        j = i % steps
        return (j % across, b[i // steps] + j // across, 0)

    specs = [pl.BlockSpec((lines, sites, orbitals), piece_at(p)) for p in range(parts)]
    specs.append(pl.BlockSpec((orbitals, orbitals), lambda i, b: (0, 0)))
    operands = [*pieces, inverse]
    aliases = {}
    if result is not None:
        specs.append(pl.BlockSpec(memory_space=pl.ANY))
        operands.append(result)
        aliases = {parts + 2: 0}
    return pl.pallas_call(
        functools.partial(out_body, parts, steps, lines, sites),
        grid_spec=pltpu.PrefetchScalarGridSpec(
            num_scalar_prefetch=1,
            grid=(parts * steps,),
            in_specs=specs,
            out_specs=pl.BlockSpec((sites, lines, orbitals), out_at),
            scratch_shapes=[
                pltpu.VMEM((lines, sites, orbitals), jnp.bfloat16),
                pltpu.VMEM((orbitals // LANES, lines * sites, LANES), jnp.float32),
            ],
        ),
        out_shape=jax.ShapeDtypeStruct(shape, jnp.bfloat16),
        input_output_aliases=aliases,
        compiler_params=pltpu.CompilerParams(vmem_limit_bytes=VMEM),
        cost_estimate=pl.CostEstimate(
            flops=2 * parts * rows * own * orbitals * orbitals,
            bytes_accessed=4 * parts * rows * own * orbitals,
            transcendentals=0,
        ),
        name="orthonormal_rows",
    )(jnp.stack(bases) // lines, *operands)


def times(left, right):
    return jnp.dot(left, right, precision=lax.Precision.HIGHEST, preferred_element_type=jnp.float32)


def small_inverse(lower):
    identity = jnp.eye(lower.shape[-1], dtype=jnp.float32)
    return jax.scipy.linalg.solve_triangular(lower, identity, lower=True)


def factorize(gram):
    half = gram.shape[-1] // 2
    upper = jnp.zeros((half, half), jnp.float32)
    first = jnp.linalg.cholesky(gram[:half, :half])
    first_inverse = small_inverse(first)
    below = times(gram[half:, :half], first_inverse.T)
    second = jnp.linalg.cholesky(gram[half:, half:] - times(below, below.T))
    second_inverse = small_inverse(second)
    corner = -times(second_inverse, times(below, first_inverse))
    lower = jnp.block([[first, upper], [below, second]])
    inverse = jnp.block([[first_inverse.T, corner.T], [upper, second_inverse.T]])
    return lower, inverse.astype(jnp.bfloat16)


def one_walker(count, walker, field, kinetic_x, kinetic_y):
    me = lax.axis_index("site")
    own, depth, orbitals = walker.shape
    share = depth // count
    chunks = max(1, min(CHUNKS, share // TILE))
    rows = share // chunks
    lines = min(LINES, rows)
    far = [d for d in range(count) if d >= CORES]
    near = [d for d in range(count) if d < CORES]

    def swap(value, d):
        if d == 0:
            return value
        return lax.ppermute(value, "site", [(s, s ^ d) for s in range(count)])

    def base(d, c):
        return (me ^ d) * share + c * rows

    blocks = [[None] * count for _ in range(chunks)]
    sent = [None]
    for c in range(chunks):
        sent = apply_y(walker, kinetic_y, [base(d, c) for d in far], rows, sent[0])
        for d, value in zip(far, sent):
            blocks[c][d] = swap(value, d)
    pairs = [(d, c) for c in range(chunks) for d in near]
    sent = apply_y(walker, kinetic_y, [base(d, c) for d, c in pairs], rows, sent[0])
    for (d, c), value in zip(pairs, sent):
        blocks[c][d] = swap(value, d)

    fields = [
        swap(lax.dynamic_slice_in_dim(field, (me ^ d) * share, share, 1), d)
        for d in range(count)
    ]
    order = [
        lax.dynamic_slice_in_dim(kinetic_x, (me ^ d) * own, own, 0) for d in range(count)
    ]
    order = jnp.concatenate(order, axis=0)
    order = jnp.concatenate(
        [lax.dynamic_slice_in_dim(order, (me ^ d) * own, own, 1) for d in range(count)], axis=1
    )
    factor = jnp.exp(jnp.concatenate(fields, axis=0).astype(jnp.float32))
    factor = factor.reshape(count * own, share // lines, lines).swapaxes(0, 1)

    scaled, gram = [], jnp.zeros((orbitals, orbitals), jnp.float32)
    per = rows // lines
    for c in range(chunks):
        outs, gram = apply_x(blocks[c], order, factor[c * per : (c + 1) * per], gram, lines)
        scaled.append(outs)
    gram = gram * (1.0 / (count * own * depth))
    step = 1
    while step < count:
        gram = gram + swap(gram, step)
        step *= 2

    home = [[swap(scaled[c][e], e) for e in range(count)] for c in range(chunks)]
    lower, inverse = factorize(gram)
    pieces = [(c, e) for c in range(chunks) for e in near]
    late = [(c, e) for c in range(chunks) for e in far]
    cut = len(late) // 2
    result = None
    for group in [pieces + late[:cut]] + [[one] for one in late[cut:]]:
        result = orthonormal_rows(
            [home[c][e] for c, e in group], inverse, [base(e, c) for c, e in group], result, walker.shape
        )
    return result, lower


def per_device(count, walkers, fields, kinetic_x, kinetic_y):
    results, lowers = [], []
    for w in range(walkers.shape[0]):
        result, lower = one_walker(count, walkers[w], fields[w, 0], kinetic_x, kinetic_y)
        results.append(result[None])
        lowers.append(lower[None])
    return jnp.concatenate(results, axis=0), jnp.concatenate(lowers, axis=0)


def solution(mesh):
    count = mesh.shape["site"]
    placed = (
        P(("grp", "spin"), "site", None, None),
        P(("grp", "spin"), None, "site", None),
        P(),
        P(),
    )

    def body(walkers, fields, kinetic_x, kinetic_y):
        return per_device(count, walkers, fields, kinetic_x, kinetic_y)

    step = jax.shard_map(
        body,
        mesh=mesh,
        in_specs=placed,
        out_specs=(P(("grp", "spin"), "site", None, None), P(("grp", "spin"), None, None)),
        check_vma=False,
    )

    def whole(walkers, fields, kinetic_x, kinetic_y):
        chunks = max(1, min(CHUNKS, walkers.shape[2] // count // TILE))
        run = step
        if chunks > 1:
            run = step
        return run(walkers, fields, kinetic_x, kinetic_y)

    return whole
```

```python
import functools

import jax
import jax.numpy as jnp
from jax import lax
from jax.experimental import pallas as pl
from jax.experimental.pallas import tpu as pltpu
from jax.sharding import PartitionSpec as P

CORES = 2
TILE = 16
CHUNKS = 4
LINES = 4
VMEM = 48 * 1024 * 1024


def make_swap(perm):
    @pl.when(pl.program_id(0) == 0)
    def _():
        to = lax.broadcasted_iota(jnp.int32, perm.shape, 0)
        source = lax.broadcasted_iota(jnp.int32, perm.shape, 1)
        hit = (to % TILE == source // TILE) & (to // TILE == source % TILE)
        perm[...] = jnp.where(hit, 1.0, 0.0).astype(jnp.bfloat16)


def swapped(perm, value):
    return jnp.dot(perm[...], value, preferred_element_type=jnp.float32).astype(jnp.bfloat16)


def y_body(parts, rows, sites, base_ref, *refs):
    kinetic, w_ref, outs = refs[:parts], refs[parts], refs[-parts - 2 : -2]
    acc, perm = refs[-2:]
    make_swap(perm)
    left = jnp.concatenate([k[...] for k in kinetic], axis=0)
    for x in range(sites):
        value = jnp.dot(left, w_ref[x], preferred_element_type=jnp.float32)
        acc[:, x] = value.astype(jnp.bfloat16).reshape(-1, TILE, value.shape[1])
    for part in range(parts):
        for first in range(0, rows, TILE):
            group = acc[(part * rows + first) // TILE]
            done = swapped(perm, group.reshape(-1, group.shape[-1]))
            outs[part][first : first + TILE] = done.reshape(group.shape)


def apply_y(walker, kinetic, bases, rows, after):
    own, depth, orbitals = walker.shape
    parts = len(bases)
    every = rows * parts
    specs = [pl.BlockSpec((rows, depth), lambda i, b, p=p: (b[p], 0)) for p in range(parts)]
    specs.append(pl.BlockSpec((TILE, depth, orbitals), lambda i, b: (i, 0, 0)))
    operands = [kinetic] * parts + [walker]
    if after is not None:
        specs.append(pl.BlockSpec(memory_space=pl.ANY))
        operands.append(after)
    return pl.pallas_call(
        functools.partial(y_body, parts, rows, TILE),
        grid_spec=pltpu.PrefetchScalarGridSpec(
            num_scalar_prefetch=1,
            grid=(own // TILE,),
            in_specs=specs,
            out_specs=[pl.BlockSpec((rows, TILE, orbitals), lambda i, b: (0, i, 0))] * parts,
            scratch_shapes=[
                pltpu.VMEM((every // TILE, TILE, TILE, orbitals), jnp.bfloat16),
                pltpu.VMEM((TILE * TILE, TILE * TILE), jnp.bfloat16),
            ],
        ),
        out_shape=[jax.ShapeDtypeStruct((rows, own, orbitals), jnp.bfloat16)] * parts,
        compiler_params=pltpu.CompilerParams(vmem_limit_bytes=VMEM),
        cost_estimate=pl.CostEstimate(
            flops=2 * every * own * depth * orbitals,
            bytes_accessed=2 * own * orbitals * (depth + every),
            transcendentals=0,
        ),
        name="apply_y",
    )(jnp.stack(bases) // rows, *operands)


def x_body(count, lines, own, k_ref, f_ref, g_ref, *refs):
    ins, outs, gram = refs[:count], refs[count : 2 * count], refs[2 * count]

    @pl.when(pl.program_id(0) == 0)
    def _():
        gram[...] = g_ref[...]

    total = None
    for y in range(lines):
        column = jnp.concatenate([r[y] for r in ins], axis=0)
        moved = jnp.dot(k_ref[...], column, preferred_element_type=jnp.float32)
        factor = f_ref[0, :, y : y + 1]
        out = (factor * moved.astype(jnp.bfloat16).astype(jnp.float32)).astype(jnp.bfloat16)
        for e in range(count):
            outs[e][y] = out[e * own : (e + 1) * own]
        part = lax.dot_general(out, out, (((0,), (0,)), ((), ())), preferred_element_type=jnp.float32)
        total = part if total is None else total + part
    gram[...] += total


def apply_x(columns, kinetic, factor, gram, lines):
    count = len(columns)
    rows, own, orbitals = columns[0].shape
    every = count * own
    block = pl.BlockSpec((lines, own, orbitals), lambda i: (i, 0, 0))
    outs = pl.pallas_call(
        functools.partial(x_body, count, lines, own),
        grid=(rows // lines,),
        in_specs=[
            pl.BlockSpec((every, every), lambda i: (0, 0)),
            pl.BlockSpec((1, every, lines), lambda i: (i, 0, 0)),
            pl.BlockSpec((orbitals, orbitals), lambda i: (0, 0)),
        ]
        + [block] * count,
        out_specs=[block] * count + [pl.BlockSpec((orbitals, orbitals), lambda i: (0, 0))],
        out_shape=[jax.ShapeDtypeStruct((rows, own, orbitals), jnp.bfloat16)] * count
        + [jax.ShapeDtypeStruct((orbitals, orbitals), jnp.float32)],
        compiler_params=pltpu.CompilerParams(vmem_limit_bytes=VMEM),
        cost_estimate=pl.CostEstimate(
            flops=2 * rows * every * orbitals * (every + orbitals),
            bytes_accessed=4 * rows * every * orbitals,
            transcendentals=0,
        ),
        name="apply_x",
    )(kinetic, factor, gram, *columns)
    return outs[:count], outs[count]


def out_body(parts, steps, sites, base_ref, *refs):
    ins, v_ref, out, held, perm = refs[:parts], refs[parts], refs[-3], refs[-2], refs[-1]
    make_swap(perm)
    for p in range(parts):

        @pl.when(pl.program_id(0) // steps == p)
        def _(p=p):
            held[...] = ins[p][...]

    for first in range(0, sites, TILE):
        group = held[:, first : first + TILE, :]
        rows = swapped(perm, group.reshape(-1, group.shape[-1]))
        value = jnp.dot(rows, v_ref[...], preferred_element_type=jnp.float32)
        out[first : first + TILE] = value.astype(jnp.bfloat16).reshape(group.shape)


def orthonormal_rows(pieces, inverse, bases, result, shape):
    parts = len(pieces)
    rows, own, orbitals = pieces[0].shape
    lines, sites = TILE, min(own, 64)
    across = own // sites
    steps = (rows // lines) * across

    def piece_at(p):
        def at(i, b):
            j = jnp.clip(i - p * steps, 0, steps - 1)
            return (j // across, j % across, 0)

        return at

    def out_at(i, b):
        j = i % steps
        return (j % across, b[i // steps] + j // across, 0)

    specs = [pl.BlockSpec((lines, sites, orbitals), piece_at(p)) for p in range(parts)]
    specs.append(pl.BlockSpec((orbitals, orbitals), lambda i, b: (0, 0)))
    operands = [*pieces, inverse]
    aliases = {}
    if result is not None:
        specs.append(pl.BlockSpec(memory_space=pl.ANY))
        operands.append(result)
        aliases = {parts + 2: 0}
    return pl.pallas_call(
        functools.partial(out_body, parts, steps, sites),
        grid_spec=pltpu.PrefetchScalarGridSpec(
            num_scalar_prefetch=1,
            grid=(parts * steps,),
            in_specs=specs,
            out_specs=pl.BlockSpec((sites, lines, orbitals), out_at),
            scratch_shapes=[
                pltpu.VMEM((lines, sites, orbitals), jnp.bfloat16),
                pltpu.VMEM((TILE * TILE, TILE * TILE), jnp.bfloat16),
            ],
        ),
        out_shape=jax.ShapeDtypeStruct(shape, jnp.bfloat16),
        input_output_aliases=aliases,
        compiler_params=pltpu.CompilerParams(vmem_limit_bytes=VMEM),
        cost_estimate=pl.CostEstimate(
            flops=2 * parts * rows * own * orbitals * orbitals,
            bytes_accessed=4 * parts * rows * own * orbitals,
            transcendentals=0,
        ),
        name="orthonormal_rows",
    )(jnp.stack(bases) // lines, *operands)


def times(left, right):
    return jnp.dot(left, right, precision=lax.Precision.HIGHEST, preferred_element_type=jnp.float32)


def small_inverse(lower):
    identity = jnp.eye(lower.shape[-1], dtype=jnp.float32)
    return jax.scipy.linalg.solve_triangular(lower, identity, lower=True)


def factorize(gram):
    half = gram.shape[-1] // 2
    upper = jnp.zeros((half, half), jnp.float32)
    first = jnp.linalg.cholesky(gram[:half, :half])
    first_inverse = small_inverse(first)
    below = times(gram[half:, :half], first_inverse.T)
    second = jnp.linalg.cholesky(gram[half:, half:] - times(below, below.T))
    second_inverse = small_inverse(second)
    corner = -times(second_inverse, times(below, first_inverse))
    lower = jnp.block([[first, upper], [below, second]])
    inverse = jnp.block([[first_inverse.T, corner.T], [upper, second_inverse.T]])
    return lower, inverse.astype(jnp.bfloat16)


def one_walker(count, walker, field, kinetic_x, kinetic_y):
    me = lax.axis_index("site")
    own, depth, orbitals = walker.shape
    share = depth // count
    chunks = max(1, min(CHUNKS, share // TILE))
    rows = share // chunks
    lines = min(LINES, rows)
    far = [d for d in range(count) if d >= CORES]
    near = [d for d in range(count) if d < CORES]

    def swap(value, d):
        if d == 0:
            return value
        return lax.ppermute(value, "site", [(s, s ^ d) for s in range(count)])

    def base(d, c):
        return (me ^ d) * share + c * rows

    blocks = [[None] * count for _ in range(chunks)]
    sent = [None]
    for c in range(chunks):
        sent = apply_y(walker, kinetic_y, [base(d, c) for d in far], rows, sent[0])
        for d, value in zip(far, sent):
            blocks[c][d] = swap(value, d)
    pairs = [(d, c) for c in range(chunks) for d in near]
    sent = apply_y(walker, kinetic_y, [base(d, c) for d, c in pairs], rows, sent[0])
    for (d, c), value in zip(pairs, sent):
        blocks[c][d] = swap(value, d)

    fields = [
        swap(lax.dynamic_slice_in_dim(field, (me ^ d) * share, share, 1), d)
        for d in range(count)
    ]
    order = [
        lax.dynamic_slice_in_dim(kinetic_x, (me ^ d) * own, own, 0) for d in range(count)
    ]
    order = jnp.concatenate(order, axis=0)
    order = jnp.concatenate(
        [lax.dynamic_slice_in_dim(order, (me ^ d) * own, own, 1) for d in range(count)], axis=1
    )
    factor = jnp.exp(jnp.concatenate(fields, axis=0).astype(jnp.float32))
    factor = factor.reshape(count * own, share // lines, lines).swapaxes(0, 1)

    scaled, gram = [], jnp.zeros((orbitals, orbitals), jnp.float32)
    per = rows // lines
    for c in range(chunks):
        outs, gram = apply_x(blocks[c], order, factor[c * per : (c + 1) * per], gram, lines)
        scaled.append(outs)
    gram = gram * (1.0 / (count * own * depth))
    step = 1
    while step < count:
        gram = gram + swap(gram, step)
        step *= 2

    home = [[swap(scaled[c][e], e) for e in range(count)] for c in range(chunks)]
    lower, inverse = factorize(gram)
    pieces = [(c, e) for c in range(chunks) for e in near]
    late = [(c, e) for c in range(chunks) for e in far]
    cut = len(late) // 2
    result = None
    for group in [pieces + late[:cut]] + [[one] for one in late[cut:]]:
        result = orthonormal_rows(
            [home[c][e] for c, e in group], inverse, [base(e, c) for c, e in group], result, walker.shape
        )
    return result, lower


def per_device(count, walkers, fields, kinetic_x, kinetic_y):
    results, lowers = [], []
    for w in range(walkers.shape[0]):
        result, lower = one_walker(count, walkers[w], fields[w, 0], kinetic_x, kinetic_y)
        results.append(result[None])
        lowers.append(lower[None])
    return jnp.concatenate(results, axis=0), jnp.concatenate(lowers, axis=0)


def solution(mesh):
    count = mesh.shape["site"]
    placed = (
        P(("grp", "spin"), "site", None, None),
        P(("grp", "spin"), None, "site", None),
        P(),
        P(),
    )

    def body(walkers, fields, kinetic_x, kinetic_y):
        return per_device(count, walkers, fields, kinetic_x, kinetic_y)

    step = jax.shard_map(
        body,
        mesh=mesh,
        in_specs=placed,
        out_specs=(P(("grp", "spin"), "site", None, None), P(("grp", "spin"), None, None)),
        check_vma=False,
    )

    def whole(walkers, fields, kinetic_x, kinetic_y):
        chunks = max(1, min(CHUNKS, walkers.shape[2] // count // TILE))
        run = step
        if chunks > 1:
            run = step
        return run(walkers, fields, kinetic_x, kinetic_y)

    return whole
```

```python
import functools

import jax
import jax.numpy as jnp
from jax import lax
from jax.experimental import pallas as pl
from jax.experimental.pallas import tpu as pltpu
from jax.sharding import PartitionSpec as P

CORES = 2
TILE = 16
CHUNKS = 4
LINES = 4
VMEM = 48 * 1024 * 1024


def make_swap(perm):
    @pl.when(pl.program_id(0) == 0)
    def _():
        to = lax.broadcasted_iota(jnp.int32, perm.shape, 0)
        source = lax.broadcasted_iota(jnp.int32, perm.shape, 1)
        hit = (to % TILE == source // TILE) & (to // TILE == source % TILE)
        perm[...] = jnp.where(hit, 1.0, 0.0).astype(jnp.bfloat16)


def swapped(perm, value):
    return jnp.dot(perm[...], value, preferred_element_type=jnp.float32).astype(jnp.bfloat16)


def y_body(parts, rows, sites, base_ref, *refs):
    kinetic, w_ref, outs = refs[:parts], refs[parts], refs[-parts - 2 : -2]
    acc, perm = refs[-2:]
    make_swap(perm)
    left = jnp.concatenate([k[...] for k in kinetic], axis=0)
    for x in range(sites):
        value = jnp.dot(left, w_ref[x], preferred_element_type=jnp.float32)
        acc[:, x] = value.astype(jnp.bfloat16).reshape(-1, TILE, value.shape[1])
    for part in range(parts):
        for first in range(0, rows, TILE):
            group = acc[(part * rows + first) // TILE]
            done = swapped(perm, group.reshape(-1, group.shape[-1]))
            outs[part][first : first + TILE] = done.reshape(group.shape)


def apply_y(walker, kinetic, bases, rows, start, own, after):
    _, depth, orbitals = walker.shape
    parts = len(bases)
    every = rows * parts
    specs = [pl.BlockSpec((rows, depth), lambda i, b, p=p: (b[p], 0)) for p in range(parts)]
    specs.append(pl.BlockSpec((TILE, depth, orbitals), lambda i, b: (i + start // TILE, 0, 0)))
    operands = [kinetic] * parts + [walker]
    if after is not None:
        specs.append(pl.BlockSpec(memory_space=pl.ANY))
        operands.append(after)
    return pl.pallas_call(
        functools.partial(y_body, parts, rows, TILE),
        grid_spec=pltpu.PrefetchScalarGridSpec(
            num_scalar_prefetch=1,
            grid=(own // TILE,),
            in_specs=specs,
            out_specs=[pl.BlockSpec((rows, TILE, orbitals), lambda i, b: (0, i, 0))] * parts,
            scratch_shapes=[
                pltpu.VMEM((every // TILE, TILE, TILE, orbitals), jnp.bfloat16),
                pltpu.VMEM((TILE * TILE, TILE * TILE), jnp.bfloat16),
            ],
        ),
        out_shape=[jax.ShapeDtypeStruct((rows, own, orbitals), jnp.bfloat16)] * parts,
        compiler_params=pltpu.CompilerParams(vmem_limit_bytes=VMEM),
        cost_estimate=pl.CostEstimate(
            flops=2 * every * own * depth * orbitals,
            bytes_accessed=2 * own * orbitals * (depth + every),
            transcendentals=0,
        ),
        name="apply_y",
    )(jnp.stack(bases) // rows, *operands)


def x_body(count, lines, own, k_ref, f_ref, g_ref, *refs):
    ins, outs, gram = refs[: -count - 1], refs[-count - 1 : -1], refs[-1]

    @pl.when(pl.program_id(0) == 0)
    def _():
        gram[...] = g_ref[...]

    total = None
    for y in range(lines):
        column = jnp.concatenate([r[y] for r in ins], axis=0)
        moved = jnp.dot(k_ref[...], column, preferred_element_type=jnp.float32)
        factor = f_ref[0, :, y : y + 1]
        out = (factor * moved.astype(jnp.bfloat16).astype(jnp.float32)).astype(jnp.bfloat16)
        for e in range(count):
            outs[e][y] = out[e * own : (e + 1) * own]
        part = lax.dot_general(out, out, (((0,), (0,)), ((), ())), preferred_element_type=jnp.float32)
        total = part if total is None else total + part
    gram[...] += total


def apply_x(columns, kinetic, factor, gram, lines):
    count = len(columns)
    columns = [piece for pieces in columns for piece in pieces]
    rows, _, orbitals = columns[0].shape
    every = kinetic.shape[0]
    own = every // count

    def block(sites):
        return pl.BlockSpec((lines, sites, orbitals), lambda i: (i, 0, 0))

    outs = pl.pallas_call(
        functools.partial(x_body, count, lines, own),
        grid=(rows // lines,),
        in_specs=[
            pl.BlockSpec((every, every), lambda i: (0, 0)),
            pl.BlockSpec((1, every, lines), lambda i: (i, 0, 0)),
            pl.BlockSpec((orbitals, orbitals), lambda i: (0, 0)),
        ]
        + [block(column.shape[1]) for column in columns],
        out_specs=[block(own)] * count + [pl.BlockSpec((orbitals, orbitals), lambda i: (0, 0))],
        out_shape=[jax.ShapeDtypeStruct((rows, own, orbitals), jnp.bfloat16)] * count
        + [jax.ShapeDtypeStruct((orbitals, orbitals), jnp.float32)],
        compiler_params=pltpu.CompilerParams(vmem_limit_bytes=VMEM),
        cost_estimate=pl.CostEstimate(
            flops=2 * rows * every * orbitals * (every + orbitals),
            bytes_accessed=4 * rows * every * orbitals,
            transcendentals=0,
        ),
        name="apply_x",
    )(kinetic, factor, gram, *columns)
    return outs[:count], outs[count]


def out_body(parts, steps, sites, base_ref, *refs):
    ins, v_ref, out, held, perm = refs[:parts], refs[parts], refs[-3], refs[-2], refs[-1]
    make_swap(perm)
    for p in range(parts):

        @pl.when(pl.program_id(0) // steps == p)
        def _(p=p):
            held[...] = ins[p][...]

    for first in range(0, sites, TILE):
        group = held[:, first : first + TILE, :]
        rows = swapped(perm, group.reshape(-1, group.shape[-1]))
        value = jnp.dot(rows, v_ref[...], preferred_element_type=jnp.float32)
        out[first : first + TILE] = value.astype(jnp.bfloat16).reshape(group.shape)


def orthonormal_rows(pieces, inverse, bases, result, shape):
    parts = len(pieces)
    rows, own, orbitals = pieces[0].shape
    lines, sites = TILE, min(own, 64)
    across = own // sites
    steps = (rows // lines) * across

    def piece_at(p):
        def at(i, b):
            j = jnp.clip(i - p * steps, 0, steps - 1)
            return (j // across, j % across, 0)

        return at

    def out_at(i, b):
        j = i % steps
        return (j % across, b[i // steps] + j // across, 0)

    specs = [pl.BlockSpec((lines, sites, orbitals), piece_at(p)) for p in range(parts)]
    specs.append(pl.BlockSpec((orbitals, orbitals), lambda i, b: (0, 0)))
    operands = [*pieces, inverse]
    aliases = {}
    if result is not None:
        specs.append(pl.BlockSpec(memory_space=pl.ANY))
        operands.append(result)
        aliases = {parts + 2: 0}
    return pl.pallas_call(
        functools.partial(out_body, parts, steps, sites),
        grid_spec=pltpu.PrefetchScalarGridSpec(
            num_scalar_prefetch=1,
            grid=(parts * steps,),
            in_specs=specs,
            out_specs=pl.BlockSpec((sites, lines, orbitals), out_at),
            scratch_shapes=[
                pltpu.VMEM((lines, sites, orbitals), jnp.bfloat16),
                pltpu.VMEM((TILE * TILE, TILE * TILE), jnp.bfloat16),
            ],
        ),
        out_shape=jax.ShapeDtypeStruct(shape, jnp.bfloat16),
        input_output_aliases=aliases,
        compiler_params=pltpu.CompilerParams(vmem_limit_bytes=VMEM),
        cost_estimate=pl.CostEstimate(
            flops=2 * parts * rows * own * orbitals * orbitals,
            bytes_accessed=4 * parts * rows * own * orbitals,
            transcendentals=0,
        ),
        name="orthonormal_rows",
    )(jnp.stack(bases) // lines, *operands)


def times(left, right):
    return jnp.dot(left, right, precision=lax.Precision.HIGHEST, preferred_element_type=jnp.float32)


def small_inverse(lower):
    identity = jnp.eye(lower.shape[-1], dtype=jnp.float32)
    return jax.scipy.linalg.solve_triangular(lower, identity, lower=True)


def factorize(gram):
    half = gram.shape[-1]
    top, side, bottom = gram[:half], gram[half : 2 * half], gram[2 * half :]
    upper = jnp.zeros((half, half), jnp.float32)
    first = jnp.linalg.cholesky(top)
    first_inverse = small_inverse(first)
    below = times(side, first_inverse.T)
    second = jnp.linalg.cholesky(bottom - times(below, below.T))
    second_inverse = small_inverse(second)
    corner = -times(second_inverse, times(below, first_inverse))
    lower = jnp.block([[first, upper], [below, second]])
    inverse = jnp.block([[first_inverse.T, corner.T], [upper, second_inverse.T]])
    return lower, inverse.astype(jnp.bfloat16)


def one_walker(count, walker, field, kinetic_x, kinetic_y):
    me = lax.axis_index("site")
    own, depth, orbitals = walker.shape
    share = depth // count
    chunks = max(1, min(CHUNKS, share // TILE))
    rows = share // chunks
    lines = min(LINES, rows)
    far = [d for d in range(count) if d >= CORES]
    near = [d for d in range(count) if d < CORES]

    def swap(value, d):
        if d == 0:
            return value
        return lax.ppermute(value, "site", [(s, s ^ d) for s in range(count)])

    def base(d, c):
        return (me ^ d) * share + c * rows

    blocks = [[[] for _ in range(count)] for _ in range(chunks)]
    sent = [None]
    for c, start, sites in early_pieces(own, chunks):
        sent = apply_y(walker, kinetic_y, [base(d, c) for d in far], rows, start, sites, sent[0])
        for d, value in zip(far, sent):
            blocks[c][d].append(swap(value, d))
    pairs = [(d, c) for c in range(chunks) for d in near]
    sent = apply_y(walker, kinetic_y, [base(d, c) for d, c in pairs], rows, 0, own, sent[0])
    for (d, c), value in zip(pairs, sent):
        blocks[c][d].append(swap(value, d))

    fields = [
        swap(lax.dynamic_slice_in_dim(field, (me ^ d) * share, share, 1), d)
        for d in range(count)
    ]
    order = [
        lax.dynamic_slice_in_dim(kinetic_x, (me ^ d) * own, own, 0) for d in range(count)
    ]
    order = jnp.concatenate(order, axis=0)
    order = jnp.concatenate(
        [lax.dynamic_slice_in_dim(order, (me ^ d) * own, own, 1) for d in range(count)], axis=1
    )
    factor = jnp.exp(jnp.concatenate(fields, axis=0).astype(jnp.float32))
    factor = factor.reshape(count * own, share // lines, lines).swapaxes(0, 1)

    scaled, gram = [], jnp.zeros((orbitals, orbitals), jnp.float32)
    per = rows // lines
    for c in range(chunks):
        outs, gram = apply_x(blocks[c], order, factor[c * per : (c + 1) * per], gram, lines)
        scaled.append(outs)
    gram = gram * (1.0 / (count * own * depth))
    half = orbitals // 2
    gram = jnp.concatenate([gram[:half, :half], gram[half:, :half], gram[half:, half:]], axis=0)
    gram = gram + swap(gram, 1)
    core = me % CORES
    size = gram.shape[0] // CORES
    mine = lax.dynamic_slice_in_dim(gram, core * size, size, 0)
    step = CORES
    while step < count:
        arrived = swap(mine, step)
        mine = mine + arrived
        step *= 2
    other = swap(mine, 1)
    gram = jnp.where(
        core == 0,
        jnp.concatenate([mine, other], axis=0),
        jnp.concatenate([other, mine], axis=0),
    )

    home = [[swap(scaled[c][e], e) for e in range(count)] for c in range(chunks)]
    lower, inverse = factorize(gram)
    pieces = [(c, e) for c in range(chunks) for e in near]
    late = [(c, e) for c in range(chunks) for e in far]
    cut = len(late) // 2
    result = None
    for group in [pieces + late[:cut]] + [[one] for one in late[cut:]]:
        result = orthonormal_rows(
            [home[c][e] for c, e in group], inverse, [base(e, c) for c, e in group], result, walker.shape
        )
    return result, lower


def per_device(count, walkers, fields, kinetic_x, kinetic_y):
    results, lowers = [], []
    for w in range(walkers.shape[0]):
        result, lower = one_walker(count, walkers[w], fields[w, 0], kinetic_x, kinetic_y)
        results.append(result[None])
        lowers.append(lower[None])
    return jnp.concatenate(results, axis=0), jnp.concatenate(lowers, axis=0)


def early_pieces(own, chunks):
    cut = own // 4
    whole = [(c, 0, own) for c in range(chunks)]
    return ([(0, 0, cut), (0, cut, own - cut)] + whole[1:]) if cut % TILE == 0 else whole


def solution(mesh):
    count = mesh.shape["site"]
    placed = (
        P(("grp", "spin"), "site", None, None),
        P(("grp", "spin"), None, "site", None),
        P(),
        P(),
    )

    def body(walkers, fields, kinetic_x, kinetic_y):
        return per_device(count, walkers, fields, kinetic_x, kinetic_y)

    step = jax.shard_map(
        body,
        mesh=mesh,
        in_specs=placed,
        out_specs=(P(("grp", "spin"), "site", None, None), P(("grp", "spin"), None, None)),
        check_vma=False,
    )

    def whole(walkers, fields, kinetic_x, kinetic_y):
        chunks = max(1, min(CHUNKS, walkers.shape[2] // count // TILE))
        run = step
        if chunks > 1:
            run = step
        return run(walkers, fields, kinetic_x, kinetic_y)

    return whole
```
